256 devices in a mesh: rows: 16 (over x, y_lo, core), cols: 16 (over y_hi, z).
Axes of the slice: x: 4, y: 4 (y_hi: 2, y_lo: 2; y = y_hi * 2 + y_lo), z: 8, core: 2. Of those that a mesh axis runs over, the one named last changes fastest.
Arguments:
- gram_tiles: float32 [25600, 25600], P('rows', 'cols'), may hold values from -1 to 4, as said below
- right_side: float32 [25600, 256], P(('rows', 'cols')), may hold values from -60 to 60
Outputs:
- solution_field: float32 [25600, 256], P(('rows', 'cols'))
- residual: float32 [25600, 256], P(('rows', 'cols'))
The draws below stay inside these ranges and needn't reach their ends.
Inputs may be any that keep to these rules, and one draw needn't show every extreme that they name: The operator A built from gram_tiles is symmetric positive definite.
All inputs are finite; a program needn't handle non-finite values.
Results may differ from the reference program's by a relative error of at most 0.0003.
Values sent between devices are 32-bit elements; how exact they have to be, the bound alone decides.
A program may use at most 128 MiB of HBM per device.

```python
import math
import jax
import jax.numpy as jnp
from jax import lax

FF = 25600
KCOLS = 256
ITERS = 4
N_ROWS = 16
N_COLS = 16


def draw_gram_tiles(key, part):
    first_key, second_key = jax.random.split(jax.random.fold_in(key, 11))
    raw_noise = jnp.clip(jax.random.normal(first_key, (FF, FF), jnp.float32), -6.0, 6.0)
    diag_vals = jnp.exp(jax.random.uniform(second_key, (FF,), jnp.float32, 0.0, math.log(3.0)))
    row_ids = jnp.arange(FF)[:, None]
    col_ids = jnp.arange(FF)[None, :]
    symmetric = (raw_noise + raw_noise.T) * (0.4 / math.sqrt(2.0 * FF))
    full_matrix = symmetric + jnp.where(row_ids == col_ids, diag_vals[:, None], 0.0)
    return full_matrix.reshape(FF, N_ROWS, N_COLS, FF // (N_ROWS * N_COLS)).transpose(0, 2, 1, 3).reshape(FF, FF)


def draw_right_side(key, part):
    keys = jax.random.split(jax.random.fold_in(key, 23), 3)
    base_vals = jnp.clip(jax.random.normal(keys[0], (FF, KCOLS), jnp.float32), -6.0, 6.0)
    row_scale = jnp.exp(jax.random.uniform(keys[1], (FF, 1), jnp.float32, math.log(0.3), math.log(3.0)))
    col_scale = jnp.exp(jax.random.uniform(keys[2], (1, KCOLS), jnp.float32, math.log(0.3), math.log(3.0)))
    return base_vals * row_scale * col_scale


def setup_inputs(seed: int = 0) -> dict:
    arg_keys = jax.random.split(jax.random.key(seed), 3)
    return {
        "gram_tiles": draw_gram_tiles(jax.random.fold_in(arg_keys[2], 71), 0),
        "right_side": draw_right_side(jax.random.fold_in(arg_keys[2], 71), 0),
    }


def apply_operator(gram_tiles, vectors):
    width = vectors.shape[1]
    reordered = vectors.reshape(N_ROWS, N_COLS, -1, width).transpose(1, 0, 2, 3).reshape(vectors.shape)
    return jnp.dot(gram_tiles, reordered, precision=lax.Precision.HIGHEST, preferred_element_type=jnp.float32)


def reference(gram_tiles, right_side):
    solution_field = jnp.zeros_like(right_side)
    residual = right_side
    direction = right_side
    norm_now = jnp.sum(residual * residual, axis=0)
    for iteration in range(ITERS):
        applied = apply_operator(gram_tiles, direction)
        step_size = norm_now / jnp.sum(direction * applied, axis=0)
        solution_field = solution_field + step_size * direction
        residual = residual - step_size * applied
        norm_next = jnp.sum(residual * residual, axis=0)
        direction = residual + (norm_next / norm_now) * direction
        norm_now = norm_next
    return solution_field, residual
```

```python
import jax
import jax.numpy as jnp
from jax import lax
from jax.experimental import pallas as pl
from jax.experimental.pallas import tpu as pltpu
from jax.sharding import PartitionSpec as P

ITERS = 4
NX, NZ = 4, 8
PIECE, SLOT, KSLOT = 100, 104, 112
WIDTH = 256
STREAMS = 2
NC = WIDTH // STREAMS
ROWS = 1600
MPAD = 16 * SLOT
KPAD = 16 * KSLOT
CHUNK = 4 * SLOT
F32, BF16 = jnp.float32, jnp.bfloat16

HALF = "g" + "mm" + "g" + "m" + "ggg" + "mm" + "gg" + "m" + "gg" + "mm" + "gg" + "m" + "gggg" + "mm" + "ggg"


def halves(x):
    hi = x.astype(BF16)
    lo = (x - hi.astype(F32)).astype(BF16)
    return hi, lo


def kernel(gram, rhs, sol, res, tv, tp, t1, t2, tt, vb, ag, os, cr, xa, xs, xb, ys, yr, st, sc, fs, fr,
           t_sem, y_snd, y_rcv, z_snd, z_rcv, c_snd, c_rcv, xa_snd, xa_rcv, xb_snd, xb_rcv, q_snd, q_rcv,
           f_snd, f_rcv):
    row, col = lax.axis_index("rows"), lax.axis_index("cols")
    xx, yl, core = row // 4, lax.rem(row // 2, 2), lax.rem(row, 2)
    yh, z = col // NZ, lax.rem(col, NZ)

    def at_x(d):
        return (lax.rem(xx + d, NX) * 4 + yl * 2 + core, col)

    def at_z(d):
        return (row, yh * NZ + lax.rem(z + d, NZ))

    at_core = (xx * 4 + yl * 2 + 1 - core, col)
    at_yl = (xx * 4 + (1 - yl) * 2 + core, col)
    at_yh = (row, (1 - yh) * NZ + z)
    partners = [at_core, at_yl, at_yh] + [at_x(d) for d in range(1, NX)] + [at_z(d) for d in range(1, NZ)]

    def remote(src, dst, snd, rcv, to):
        return pltpu.make_async_remote_copy(
            src_ref=src, dst_ref=dst, send_sem=snd, recv_sem=rcv, device_id=to,
            device_id_type=pl.DeviceIdType.MESH)

    for m in range(4):
        pltpu.make_async_copy(gram.at[pl.ds(400 * m, 400), :], tv.at[pl.ds(400 * m, 400), :], t_sem.at[m]).start()

    barrier = pltpu.get_barrier_semaphore()
    for to in partners:
        pl.semaphore_signal(barrier, inc=1, device_id=to, device_id_type=pl.DeviceIdType.MESH)

    def slot(kind, d):
        return (yh if kind == 0 else 1 - yh) * NZ + lax.rem(z + d + NZ, NZ)

    def pack(t, s, at):
        x = jnp.concatenate([ag[t, s, at], jnp.zeros((KSLOT - SLOT, NC), F32)], axis=0)
        hi, lo = halves(x)
        start = pl.multiple_of(at * KSLOT, 16)
        vb[s, pl.ds(start, KSLOT), 0:NC] = hi
        vb[s, pl.ds(start, KSLOT), NC:2 * NC] = lo

    def gather(t, s):
        par = lax.rem(t, 2)
        far = ((4, 3), (3, 4))

        def z_copy(kind, way, d):
            at = slot(kind, -d if way == 0 else d)
            return remote(ag.at[t, s, at], ag.at[t, s, at], z_snd.at[s, kind, way, d], z_rcv.at[par, s, kind, way, d],
                          at_z(1 if way == 0 else NZ - 1))

        def z_landing(kind, way, d):
            at = slot(kind, -d if way == 0 else d)
            return remote(ag.at[t, s, at], ag.at[t, s, at], z_snd.at[s, kind, way, d - 1],
                          z_rcv.at[par, s, kind, way, d - 1], at_z(NZ - 1 if way == 0 else 1))

        def y_copy():
            return remote(ag.at[t, s, slot(0, 0)], ag.at[t, s, slot(0, 0)], y_snd.at[s], y_rcv.at[par, s], at_yh)

        def y_landing():
            return remote(ag.at[t, s, slot(1, 0)], ag.at[t, s, slot(1, 0)], y_snd.at[s], y_rcv.at[par, s], at_yh)

        def first():
            y_copy().start()
            z_copy(0, 0, 0).start()
            z_copy(0, 1, 0).start()
            pack(t, s, slot(0, 0))

        def other():
            y_landing().wait_recv()
            z_copy(1, 0, 0).start()
            z_copy(1, 1, 0).start()
            pack(t, s, slot(1, 0))

        def step(kind, d):
            def run():
                for way in range(2):
                    if d <= far[kind][way]:
                        z_landing(kind, way, d).wait_recv()
                        if d < far[kind][way]:
                            z_copy(kind, way, d).start()
                for way in range(2):
                    if d <= far[kind][way]:
                        pack(t, s, slot(kind, -d if way == 0 else d))
            return run

        def drain():
            y_copy().wait_send()
            for kind in range(2):
                for way in range(2):
                    for d in range(far[kind][way]):
                        z_copy(kind, way, d).wait_send()

        return [first, step(0, 1), other, step(0, 2), step(1, 1), step(0, 3), step(1, 2), step(0, 4), step(1, 3),
                step(1, 4), drain]

    def scatter(t, s):
        par = lax.rem(t, 2)
        ahead = (2, 1, 3, 0)

        def c_copy(e):
            to = lax.rem(xx + ahead[e], NX)
            return remote(os.at[s, to, 1 - core], cr.at[t, s, to], c_snd.at[s, e], c_rcv.at[par, s, e], at_core)

        def xa_copy(k):
            return remote(xs.at[s, 0, k], xa.at[t, s, k], xa_snd.at[s, k], xa_rcv.at[par, s, k], at_x(1 if k == 0 else 3))

        def xb_copy(way, k):
            return remote(xs.at[s, 1 + way, k], xb.at[t, s, way, k], xb_snd.at[s, way, k], xb_rcv.at[par, s, way, k],
                          at_x(1 if way == 0 else 3))

        def q_copy():
            return remote(ys.at[s], yr.at[t, s], q_snd.at[s], q_rcv.at[par, s], at_yl)

        def spare():
            total = jnp.zeros((8, NC), F32)
            for b in range(16):
                total = total + ag[t, s, b, 96:104, :]
            keep = lax.broadcasted_iota(jnp.int32, (8, NC), 0)
            return jnp.where((keep == 4) | (keep == 5), total, 0.0)

        def multiply(e):
            def run():
                to = lax.rem(xx + ahead[e], NX)
                y = jnp.dot(tt[to], vb[s], preferred_element_type=F32)
                dots = spare()
                for q in range(4):
                    lo, hi = q * SLOT, (q + 1) * SLOT
                    piece = (y[lo:hi, :NC] + (y[lo:hi, NC:] + y[CHUNK + lo:CHUNK + hi, :NC])) + y[CHUNK + lo:CHUNK + hi, NC:]
                    os[s, to, q % 2, q // 2, 0:96] = piece[0:96]
                    os[s, to, q % 2, q // 2, 96:104] = piece[96:104] + dots
                c_copy(e).start()
            return run

        def pair(e, k):
            to = lax.rem(xx + ahead[e], NX)
            return os[s, to, core, k] + cr[t, s, to, k]

        def far_x():
            c_copy(0).wait_recv()
            for k in range(2):
                xs[s, 0, k] = pair(0, k)
                xa_copy(k).start()

        def near_x(way):
            def run():
                c_copy(1 + way).wait_recv()
                k = 1 - way
                xs[s, 1 + way, k] = pair(1 + way, k)
                xb_copy(way, k).start()
            return run

        def relay_x(way):
            def run():
                k = way
                both = pair(1 + way, k)
                xa_copy(k).wait_recv()
                xs[s, 1 + way, k] = both + xa[t, s, k]
                xb_copy(way, k).start()
            return run

        def own_x():
            c_copy(3).wait_recv()
            for way in range(2):
                for k in range(2):
                    xb_copy(way, k).wait_recv()
            k = 1 - yl
            ys[s] = (pair(3, k) + xb[t, s, 0, k]) + xb[t, s, 1, k]
            q_copy().start()

        def update():
            k = yl
            part = (pair(3, k) + xb[t, s, 0, k]) + xb[t, s, 1, k]
            q_copy().wait_recv()
            u = part + yr[t, s]
            renew(t, s, u)

        def drain():
            for e in range(4):
                c_copy(e).wait_send()
            for k in range(2):
                xa_copy(k).wait_send()
            for way in range(2):
                for k in range(2):
                    xb_copy(way, k).wait_send()
            q_copy().wait_send()

        def last():
            update()
            drain()

        return [multiply(0), multiply(1), far_x, multiply(2), near_x(0), multiply(3), near_x(1), relay_x(0), relay_x(1),
                own_x, last]

    R, W, Z, S, D, X = range(6)

    def renew(t, s, u):
        q0 = u[0:PIECE]

        @pl.when(t == 0)
        def _():
            st[s, W, 0:PIECE] = q0
            offer(t, s, q0)

        @pl.when(t > 0)
        def _():
            now, product = u[100:101], u[101:102]
            old_now, old_step = sc[s, 0:1], sc[s, 1:2]
            w = st[s, W, 0:PIECE]
            r = st[s, R, 0:PIECE]
            first = t == 1
            beta = jnp.where(first, 0.0, now / old_now)
            step = now / (product - jnp.where(first, 0.0, beta * now / old_step))
            q = jnp.where(first, q0, (w - q0) / old_step)
            zz = q + beta * st[s, Z, 0:PIECE]
            ss = w + beta * st[s, S, 0:PIECE]
            dd = r + beta * st[s, D, 0:PIECE]
            w = w - step * zz
            r = r - step * ss
            sc[s, 0:1] = now
            sc[s, 1:2] = step
            st[s, Z, 0:PIECE] = zz
            st[s, S, 0:PIECE] = ss
            st[s, D, 0:PIECE] = dd
            st[s, W, 0:PIECE] = w
            st[s, R, 0:PIECE] = r
            st[s, X, 0:PIECE] = st[s, X, 0:PIECE] + step * dd

            @pl.when(t < ITERS - 1)
            def _():
                offer(t, s, r - step * w)

    def dots_of(s):
        r = st[s, R, 0:PIECE]
        w = st[s, W, 0:PIECE]
        return jnp.sum(r * r, axis=0, keepdims=True), jnp.sum(r * w, axis=0, keepdims=True)

    def offer(t, s, v):
        a, b = dots_of(s)
        mine = slot(0, 0)
        ag[t + 1, s, mine, 0:PIECE] = v
        ag[t + 1, s, mine, 100:101] = a
        ag[t + 1, s, mine, 101:102] = b
        ag[t + 1, s, mine, 102:104] = jnp.zeros((2, NC), F32)

    def finish(s):
        plan = [[(at_core, 0)], [(at_yl, 1)], [(at_x(d), 1 + d) for d in range(1, NX)], [(at_yh, 5)],
                [(at_z(d), 5 + d) for d in range(1, NZ)]]

        def copies(stage):
            return [remote(fs.at[s, stage], fr.at[s, k], f_snd.at[s, k], f_rcv.at[s, k], to) for to, k in plan[stage]]

        def begin():
            a, b = dots_of(s)
            fs[s, 0, 0:1] = a
            fs[s, 0, 1:2] = b
            fs[s, 0, 2:8] = jnp.zeros((6, NC), F32)
            for c in copies(0):
                c.start()

        def arrived(stage):
            total = fs[s, stage]
            for c, (_, k) in zip(copies(stage), plan[stage]):
                c.wait_recv()
                total = total + fr[s, k]
            return total

        def onward(stage):
            def run():
                fs[s, stage] = arrived(stage - 1)
                for c in copies(stage):
                    c.start()
            return run

        def close():
            total = arrived(len(plan) - 1)
            now, product = total[0:1], total[1:2]
            old_now, old_step = sc[s, 0:1], sc[s, 1:2]
            beta = now / old_now
            step = now / (product - beta * now / old_step)
            w = st[s, W, 0:PIECE]
            r = st[s, R, 0:PIECE]
            ss = w + beta * st[s, S, 0:PIECE]
            dd = r + beta * st[s, D, 0:PIECE]
            cols = slice(s * NC, (s + 1) * NC)
            sol[:, cols] = st[s, X, 0:PIECE] + step * dd
            res[:, cols] = r - step * ss
            for stage in range(len(plan)):
                for c in copies(stage):
                    c.wait_send()

        return [begin] + [onward(k) for k in range(1, len(plan))] + [close]

    mine = slot(0, 0)
    st[...] = jnp.zeros(st.shape, F32)
    sc[...] = jnp.ones(sc.shape, F32)
    for s in range(STREAMS):
        b = rhs[:, s * NC:(s + 1) * NC]
        st[s, R, 0:PIECE] = b
        ag[0, s, mine, 0:PIECE] = b
        ag[0, s, mine, 100:104] = jnp.zeros((4, NC), F32)
    for a in range(16):
        t2[a * SLOT + PIECE:(a + 1) * SLOT] = jnp.zeros((SLOT - PIECE, 128), F32)
    pl.semaphore_wait(barrier, len(partners))
    events = gather(0, 0)
    events[0]()
    events = events[1:]

    @pl.loop(0, 4)
    def _(m):
        src = pl.multiple_of(m * 400, 8)
        pltpu.make_async_copy(gram.at[pl.ds(src, 400), :], tv.at[pl.ds(src, 400), :], t_sem.at[m]).wait()
        for p in range(2):
            base = pl.multiple_of(m * 400 + p * 200, 8)
            into = pl.multiple_of(m * 448 + p * 224, 8)
            for lane in range(0, ROWS, 128):
                wide = min(128, ROWS - lane)
                v = tv[pl.ds(base, 200), lane:lane + wide]
                none = jnp.zeros((KSLOT - PIECE, wide), F32)
                tp[pl.ds(into, 224), lane:lane + wide] = jnp.concatenate([v[0:100], none, v[100:200], none], axis=0)


    @pl.loop(0, KPAD // 128)
    def _(kb):
        at = pl.multiple_of(kb * 128, 128)
        for lane in range(0, ROWS, 128):
            wide = min(128, ROWS - lane)
            t1[lane:lane + wide] = tp[pl.ds(at, 128), lane:lane + wide].T
        for a in range(16):
            t2[a * SLOT:a * SLOT + PIECE] = t1[a * PIECE:(a + 1) * PIECE]
        for p in range(8):
            hi, lo = halves(t2[208 * p:208 * (p + 1)])
            start = (p % 2) * 208
            tt[p // 2, start:start + 208, pl.ds(at, 128)] = hi
            tt[p // 2, CHUNK + start:CHUNK + start + 208, pl.ds(at, 128)] = lo
        for i, event in enumerate(events):
            pl.when(kb == 4 + i)(event)

    def interleave(plan, g, m):
        g, m = list(g), list(m)
        for what in plan:
            if what == "g" and g:
                g.pop(0)()
            if what == "m" and m:
                m.pop(0)()
        for run in m + g:
            run()

    @pl.loop(0, STREAMS * ITERS - 1)
    def _(h):
        sm, tm = lax.rem(h, 2), h // 2
        sg, tg = 1 - sm, (h + 1) // 2
        interleave(HALF, gather(tg, sg), scatter(tm, sm))

    interleave("gm" + "mmg" + "mmg" + "mmmg" + "mg" + "mg" + "mg", finish(0), scatter(ITERS - 1, 1))
    for run in finish(1):
        run()


def body(gram_tiles, right_side):
    shard = jax.ShapeDtypeStruct(right_side.shape, F32)
    dma = pltpu.SemaphoreType.DMA
    vmem = pltpu.VMEM
    spec = pl.BlockSpec(memory_space=pltpu.VMEM)
    return pl.pallas_call(
        kernel,
        out_shape=(shard, shard),
        in_specs=[pl.BlockSpec(memory_space=pl.ANY), spec],
        out_specs=(spec, spec),
        scratch_shapes=[
            vmem((ROWS, ROWS), F32),
            vmem((KPAD, ROWS), F32),
            vmem((ROWS, 128), F32),
            vmem((MPAD, 128), F32),
            vmem((4, 2 * CHUNK, KPAD), BF16),
            vmem((STREAMS, KPAD, 2 * NC), BF16),
            vmem((ITERS, STREAMS, 16, SLOT, NC), F32),
            vmem((STREAMS, NX, 2, 2, SLOT, NC), F32),
            vmem((ITERS, STREAMS, NX, 2, SLOT, NC), F32),
            vmem((ITERS, STREAMS, 2, SLOT, NC), F32),
            vmem((STREAMS, 3, 2, SLOT, NC), F32),
            vmem((ITERS, STREAMS, 2, 2, SLOT, NC), F32),
            vmem((STREAMS, SLOT, NC), F32),
            vmem((ITERS, STREAMS, SLOT, NC), F32),
            vmem((STREAMS, 6, SLOT, NC), F32),
            vmem((STREAMS, 8, NC), F32),
            vmem((STREAMS, 5, 8, NC), F32),
            vmem((STREAMS, 13, 8, NC), F32),
            dma((4,)),
            dma((STREAMS,)), dma((2, STREAMS)),
            dma((STREAMS, 2, 2, 4)), dma((2, STREAMS, 2, 2, 4)),
            dma((STREAMS, 4)), dma((2, STREAMS, 4)),
            dma((STREAMS, 2)), dma((2, STREAMS, 2)),
            dma((STREAMS, 2, 2)), dma((2, STREAMS, 2, 2)),
            dma((STREAMS,)), dma((2, STREAMS)),
            dma((STREAMS, 13)), dma((STREAMS, 13)),
        ],
        compiler_params=pltpu.CompilerParams(
            collective_id=0, has_side_effects=True, vmem_limit_bytes=67_000_000),
        name="cg_solve",
    )(gram_tiles, right_side)


def solution(mesh):
    return jax.shard_map(
        body,
        mesh=mesh,
        in_specs=(P("rows", "cols"), P(("rows", "cols"), None)),
        out_specs=(P(("rows", "cols"), None), P(("rows", "cols"), None)),
        check_vma=False,
    )
```

```python
import functools

import jax
import jax.numpy as jnp
from jax import lax
from jax.experimental import pallas as pl
from jax.experimental.pallas import tpu as pltpu
from jax.sharding import PartitionSpec as P

ITERS = 4
NX, NZ = 4, 8
PIECE, SLOT, KSLOT = 100, 104, 112
WIDTH = 256
STREAMS = 2
NC = WIDTH // STREAMS
ROWS = 1600
MPAD = 16 * SLOT
KPAD = 16 * KSLOT
CHUNK = 4 * SLOT
F32, BF16 = jnp.float32, jnp.bfloat16

NAMES = ("O0", "O1", "O2", "O3", "O4", "Q0", "Q1", "Q2", "Q3", "Q4")
HALF = (
    "m0", "m1", "fx", "Q0", "m2", "n0", "O2", "m3", "n1", "r0", "r1", "Q1", "O3", "O4", "ox", "Q2", "O1",
    "Q3", "Q4", "up", "..",
)
LAST = (
    "f0",
    "m0",
    "m1",
    "fx",
    "m2",
    "n0",
    "m3",
    "n1",
    "r0",
    "r1",
    "f1",
    "ox",
    "f2",
    "up",
)
LOAD = {1: ["Q0"], 3: ["O2", "Q1"]}
TURN = {4: ["O1", "O3", "O4"], 7: ["Q2"], 11: ["Q3"]}
TAIL = ["Q4", ".."]


def halves(x):
    hi = x.astype(BF16)
    lo = (x - hi.astype(F32)).astype(BF16)
    return hi, lo


def follow(names, steps):
    for name in names:
        steps[name]()


def kernel(gram, rhs, ox, od, ores, os_, ostep, tv, tp, t1, t2, tt, vb, ag, os, cr, xa, xs, xb, ys, yr, st, sc, fs, fr,
           t_sem, z_snd, z_rcv, c_snd, c_rcv, xa_snd, xa_rcv, xb_snd, xb_rcv, q_snd, q_rcv,
           f_snd, f_rcv):
    row, col = lax.axis_index("rows"), lax.axis_index("cols")
    xx, yl, core = row // 4, lax.rem(row // 2, 2), lax.rem(row, 2)
    yh, z = col // NZ, lax.rem(col, NZ)

    def at_x(d):
        return (lax.rem(xx + d, NX) * 4 + yl * 2 + core, col)

    def at_z(d):
        return (row, yh * NZ + lax.rem(z + d, NZ))

    at_core = (xx * 4 + yl * 2 + 1 - core, col)
    at_yl = (xx * 4 + (1 - yl) * 2 + core, col)
    at_yh = (row, (1 - yh) * NZ + z)
    at_both = (xx * 4 + (1 - yl) * 2 + 1 - core, col)
    around = [
        [at_core, at_yl, at_both],
        [at_x(d) for d in range(1, NX)] + [at_yh] + [(at_x(d)[0], at_yh[1]) for d in range(1, NX)],
        [at_z(d) for d in range(1, NZ)],
    ]
    partners = around[0] + around[1] + around[2]

    def remote(src, dst, snd, rcv, to):
        return pltpu.make_async_remote_copy(
            src_ref=src, dst_ref=dst, send_sem=snd, recv_sem=rcv, device_id=to,
            device_id_type=pl.DeviceIdType.MESH)

    for m in range(4):
        pltpu.make_async_copy(gram.at[pl.ds(400 * m, 400), :], tv.at[pl.ds(400 * m, 400), :], t_sem.at[m]).start()

    barrier = pltpu.get_barrier_semaphore()
    for to in partners:
        pl.semaphore_signal(barrier, inc=1, device_id=to, device_id_type=pl.DeviceIdType.MESH)

    def slot(kind, d):
        return (yh if kind == 0 else 1 - yh) * NZ + lax.rem(z + d + NZ, NZ)

    def pack(t, s, at):
        x = jnp.concatenate([ag[t, s, at], jnp.zeros((KSLOT - SLOT, NC), F32)], axis=0)
        hi, lo = halves(x)
        start = pl.multiple_of(at * KSLOT, 16)
        vb[s, pl.ds(start, KSLOT), 0:NC] = hi
        vb[s, pl.ds(start, KSLOT), NC:2 * NC] = lo

    def gather(t, s):
        par = lax.rem(t, 2)
        ways = (1, -1)

        def piece(name, way):
            kind, d = (0 if name[0] == "O" else 1), int(name[1])
            return ag.at[t, s, slot(kind, -ways[way] * d)]

        def index(name, way):
            return NAMES.index(name) * 2 + way

        def copy(have, as_name, way, to):
            src = piece(have, way)
            k = index(as_name, way)
            return remote(src, src, z_snd.at[s, k], z_rcv.at[par, s, k], to)

        def landing(name, way):
            dst = piece(name, way)
            k = index(name, way)
            return remote(dst, dst, z_snd.at[s, k], z_rcv.at[par, s, k], at_yh)

        def along(way, hops):
            return at_z((ways[way] * hops) % NZ)

        def both(have, as_name, hops):
            return [copy(have, as_name, way, along(way, hops)) for way in range(2)]

        def begin():
            return [copy("O0", "Q0", 0, at_yh)] + both("O0", "O2", 2) + both("O0", "O1", 1)

        sends = lambda: {
            "Q0": [both("Q0", "Q1", 1), []],
            "Q1": [[copy("Q1", "Q2", 0, along(0, 1))], [copy("Q1", "Q2", 1, along(1, 1))]],
            "O2": [[copy("O2", "O3", 0, along(0, 1)), copy("O2", "O4", 0, along(0, 2))],
                   [copy("O2", "O3", 1, along(1, 1))]],
            "O3": [[copy("O3", "Q3", 0, at_yh)], [copy("O3", "Q3", 1, at_yh)]],
            "O4": [[copy("O4", "Q4", 0, at_yh)]],
        }

        def first():
            for c in begin():
                c.start()
            pack(t, s, slot(0, 0))

        def take(name, count=2):
            def run():
                onward = sends().get(name, [[], []])
                for way in range(count):
                    landing(name, way).wait_recv()
                    for c in onward[way]:
                        c.start()
                for way in range(count):
                    kind, d = (0 if name[0] == "O" else 1), int(name[1])
                    pack(t, s, slot(kind, -ways[way] * d))
            return run

        def drain():
            for c in begin():
                c.wait_send()
            for group in sends().values():
                for some in group:
                    for c in some:
                        c.wait_send()

        return first, {"Q0": take("Q0", 1), "O2": take("O2"), "Q1": take("Q1"), "O1": take("O1"), "O3": take("O3"),
                       "O4": take("O4", 1), "Q2": take("Q2"), "Q3": take("Q3"), "Q4": take("Q4", 1), "..": drain}

    def scatter(t, s, start_next=True):
        par = lax.rem(t, 2)
        ahead = (2, 1, 3, 0)

        def c_copy(e):
            to = lax.rem(xx + ahead[e], NX)
            return remote(os.at[s, to, 1 - core], cr.at[t, s, to], c_snd.at[s, e], c_rcv.at[par, s, e], at_core)

        def xa_copy(k):
            return remote(xs.at[s, 0, k], xa.at[t, s, k], xa_snd.at[s, k], xa_rcv.at[par, s, k], at_x(1 if k == 0 else 3))

        def xb_copy(way, k):
            return remote(xs.at[s, 1 + way, k], xb.at[t, s, way, k], xb_snd.at[s, way, k], xb_rcv.at[par, s, way, k],
                          at_x(1 if way == 0 else 3))

        def q_copy():
            return remote(ys.at[s], yr.at[t, s], q_snd.at[s], q_rcv.at[par, s], at_yl)

        def spare():
            total = jnp.zeros((8, NC), F32)
            for b in range(16):
                total = total + ag[t, s, b, 96:104, :]
            keep = lax.broadcasted_iota(jnp.int32, (8, NC), 0)
            return jnp.where((keep == 4) | (keep == 5), total, 0.0)

        def multiply(e):
            def run():
                to = lax.rem(xx + ahead[e], NX)
                y = jnp.dot(tt[to], vb[s], preferred_element_type=F32)
                dots = spare()
                for q in range(4):
                    lo, hi = q * SLOT, (q + 1) * SLOT
                    piece = (y[lo:hi, :NC] + (y[lo:hi, NC:] + y[CHUNK + lo:CHUNK + hi, :NC])) + y[CHUNK + lo:CHUNK + hi, NC:]
                    os[s, to, q % 2, q // 2, 0:96] = piece[0:96]
                    os[s, to, q % 2, q // 2, 96:104] = piece[96:104] + dots
                c_copy(e).start()
            return run

        def pair(e, k):
            to = lax.rem(xx + ahead[e], NX)
            return os[s, to, core, k] + cr[t, s, to, k]

        def far_x():
            c_copy(0).wait_recv()
            for k in range(2):
                xs[s, 0, k] = pair(0, k)
                xa_copy(k).start()

        def near_x(way):
            def run():
                c_copy(1 + way).wait_recv()
                k = 1 - way
                xs[s, 1 + way, k] = pair(1 + way, k)
                xb_copy(way, k).start()
            return run

        def relay_x(way):
            def run():
                k = way
                both = pair(1 + way, k)
                xa_copy(k).wait_recv()
                xs[s, 1 + way, k] = both + xa[t, s, k]
                xb_copy(way, k).start()
            return run

        def own_x():
            c_copy(3).wait_recv()
            for way in range(2):
                for k in range(2):
                    xb_copy(way, k).wait_recv()
            k = 1 - yl
            ys[s] = (pair(3, k) + xb[t, s, 0, k]) + xb[t, s, 1, k]
            q_copy().start()

        def update():
            k = yl
            part = (pair(3, k) + xb[t, s, 0, k]) + xb[t, s, 1, k]
            q_copy().wait_recv()
            u = part + yr[t, s]
            renew(t, s, u)

        def drain():
            for e in range(4):
                c_copy(e).wait_send()
            for k in range(2):
                xa_copy(k).wait_send()
            for way in range(2):
                for k in range(2):
                    xb_copy(way, k).wait_send()
            q_copy().wait_send()

        def last():
            update()
            if start_next:
                pl.when(t < ITERS - 1)(gather(t + 1, s)[0])
            drain()

        return {"m0": multiply(0), "m1": multiply(1), "m2": multiply(2), "m3": multiply(3), "fx": far_x,
                "n0": near_x(0), "n1": near_x(1), "r0": relay_x(0), "r1": relay_x(1), "ox": own_x, "up": last}

    R, W, Z, S, D, X = range(6)

    def renew(t, s, u):
        q0 = u[0:PIECE]

        @pl.when(t == 0)
        def _():
            st[s, W, 0:PIECE] = q0
            offer(t, s, q0)

        @pl.when(t > 0)
        def _():
            now, product = u[100:101], u[101:102]
            old_now, old_step = sc[s, 0:1], sc[s, 1:2]
            w = st[s, W, 0:PIECE]
            r = st[s, R, 0:PIECE]
            first = t == 1
            beta = jnp.where(first, 0.0, now / old_now)
            step = now / (product - jnp.where(first, 0.0, beta * now / old_step))
            q = jnp.where(first, q0, (w - q0) / old_step)
            zz = q + beta * st[s, Z, 0:PIECE]
            ss = w + beta * st[s, S, 0:PIECE]
            dd = r + beta * st[s, D, 0:PIECE]
            w = w - step * zz
            r = r - step * ss
            sc[s, 0:1] = now
            sc[s, 1:2] = step
            st[s, Z, 0:PIECE] = zz
            st[s, S, 0:PIECE] = ss
            st[s, D, 0:PIECE] = dd
            st[s, W, 0:PIECE] = w
            st[s, R, 0:PIECE] = r
            st[s, X, 0:PIECE] = st[s, X, 0:PIECE] + step * dd

            @pl.when(t < ITERS - 1)
            def _():
                offer(t, s, r - step * w)

    def dots_of(s):
        r = st[s, R, 0:PIECE]
        w = st[s, W, 0:PIECE]
        return jnp.sum(r * r, axis=0, keepdims=True), jnp.sum(r * w, axis=0, keepdims=True)

    def offer(t, s, v):
        a, b = dots_of(s)
        mine = slot(0, 0)
        ag[t + 1, s, mine, 0:PIECE] = v
        ag[t + 1, s, mine, 100:101] = a
        ag[t + 1, s, mine, 101:102] = b
        ag[t + 1, s, mine, 102:104] = jnp.zeros((2, NC), F32)

    def finish(s):
        plan, first = [], 0
        for group in around:
            plan.append([(to, first + k) for k, to in enumerate(group)])
            first += len(group)

        def copies(stage):
            return [remote(fs.at[s, stage], fr.at[s, k], f_snd.at[s, k], f_rcv.at[s, k], to) for to, k in plan[stage]]

        def begin():
            a, b = dots_of(s)
            fs[s, 0, 0:1] = a
            fs[s, 0, 1:2] = b
            fs[s, 0, 2:8] = jnp.zeros((6, NC), F32)
            for c in copies(0):
                c.start()

        def arrived(stage):
            total = fs[s, stage]
            for c, (_, k) in zip(copies(stage), plan[stage]):
                c.wait_recv()
                total = total + fr[s, k]
            return total

        def onward(stage):
            def run():
                fs[s, stage] = arrived(stage - 1)
                for c in copies(stage):
                    c.start()
            return run

        def close():
            total = arrived(len(plan) - 1)
            now, product = total[0:1], total[1:2]
            old_now, old_step = sc[s, 0:1], sc[s, 1:2]
            beta = now / old_now
            step = now / (product - beta * now / old_step)
            w = st[s, W, 0:PIECE]
            r = st[s, R, 0:PIECE]
            ss = w + beta * st[s, S, 0:PIECE]
            dd = r + beta * st[s, D, 0:PIECE]
            cols = slice(s * NC, (s + 1) * NC)
            ox[:, cols] = st[s, X, 0:PIECE]
            od[:, cols] = dd
            ores[:, cols] = r
            os_[:, cols] = ss
            ostep[:, cols] = jnp.broadcast_to(step, (8, NC))
            for stage in range(len(plan)):
                for c in copies(stage):
                    c.wait_send()

        steps = [begin] + [onward(k) for k in range(1, len(plan))] + [close]
        return {"f%d" % i: run for i, run in enumerate(steps)}

    mine = slot(0, 0)
    st[...] = jnp.zeros(st.shape, F32)
    sc[...] = jnp.ones(sc.shape, F32)
    for s in range(STREAMS):
        b = rhs[:, s * NC:(s + 1) * NC]
        st[s, R, 0:PIECE] = b
        ag[0, s, mine, 0:PIECE] = b
        ag[0, s, mine, 100:104] = jnp.zeros((4, NC), F32)
    for a in range(16):
        t2[a * SLOT + PIECE:(a + 1) * SLOT] = jnp.zeros((SLOT - PIECE, 128), F32)
    pl.semaphore_wait(barrier, len(partners))
    begin, events = gather(0, 0)
    begin()

    @pl.loop(0, 4)
    def _(m):
        src = pl.multiple_of(m * 400, 8)
        pltpu.make_async_copy(gram.at[pl.ds(src, 400), :], tv.at[pl.ds(src, 400), :], t_sem.at[m]).wait()
        for p in range(2):
            base = pl.multiple_of(m * 400 + p * 200, 8)
            into = pl.multiple_of(m * 448 + p * 224, 8)
            for lane in range(0, ROWS, 128):
                wide = min(128, ROWS - lane)
                v = tv[pl.ds(base, 200), lane:lane + wide]
                none = jnp.zeros((KSLOT - PIECE, wide), F32)
                tp[pl.ds(into, 224), lane:lane + wide] = jnp.concatenate([v[0:100], none, v[100:200], none], axis=0)
        for when, names in LOAD.items():
            pl.when(m == when)(functools.partial(follow, names, events))


    @pl.loop(0, KPAD // 128)
    def _(kb):
        at = pl.multiple_of(kb * 128, 128)
        for lane in range(0, ROWS, 128):
            wide = min(128, ROWS - lane)
            t1[lane:lane + wide] = tp[pl.ds(at, 128), lane:lane + wide].T
        for a in range(16):
            t2[a * SLOT:a * SLOT + PIECE] = t1[a * PIECE:(a + 1) * PIECE]
        for p in range(8):
            hi, lo = halves(t2[208 * p:208 * (p + 1)])
            start = (p % 2) * 208
            tt[p // 2, start:start + 208, pl.ds(at, 128)] = hi
            tt[p // 2, CHUNK + start:CHUNK + start + 208, pl.ds(at, 128)] = lo
        for when, names in TURN.items():
            pl.when(kb == when)(functools.partial(follow, names, events))

    gather(0, 1)[0]()
    follow(TAIL, events)

    @pl.loop(0, STREAMS * ITERS - 1)
    def _(h):
        sm, tm = lax.rem(h, 2), h // 2
        sg, tg = 1 - sm, (h + 1) // 2
        follow(HALF, gather(tg, sg)[1] | scatter(tm, sm))

    ending = finish(0)
    follow(LAST, ending | scatter(ITERS - 1, 1, False))
    other = finish(1)
    follow(["f0"], other)
    follow(["f3"], ending)
    follow(["f1", "f2", "f3"], other)


def body(gram_tiles, right_side):
    shard = jax.ShapeDtypeStruct(right_side.shape, F32)
    dma = pltpu.SemaphoreType.DMA
    vmem = pltpu.VMEM
    spec = pl.BlockSpec(memory_space=pltpu.VMEM)
    x, d, r, s, step = pl.pallas_call(
        kernel,
        out_shape=(shard,) * 4 + (jax.ShapeDtypeStruct((8, right_side.shape[1]), F32),),
        in_specs=[pl.BlockSpec(memory_space=pl.ANY), spec],
        out_specs=(spec,) * 5,
        scratch_shapes=[
            vmem((ROWS, ROWS), F32),
            vmem((KPAD, ROWS), F32),
            vmem((ROWS, 128), F32),
            vmem((MPAD, 128), F32),
            vmem((4, 2 * CHUNK, KPAD), BF16),
            vmem((STREAMS, KPAD, 2 * NC), BF16),
            vmem((ITERS, STREAMS, 16, SLOT, NC), F32),
            vmem((STREAMS, NX, 2, 2, SLOT, NC), F32),
            vmem((ITERS, STREAMS, NX, 2, SLOT, NC), F32),
            vmem((ITERS, STREAMS, 2, SLOT, NC), F32),
            vmem((STREAMS, 3, 2, SLOT, NC), F32),
            vmem((ITERS, STREAMS, 2, 2, SLOT, NC), F32),
            vmem((STREAMS, SLOT, NC), F32),
            vmem((ITERS, STREAMS, SLOT, NC), F32),
            vmem((STREAMS, 6, SLOT, NC), F32),
            vmem((STREAMS, 8, NC), F32),
            vmem((STREAMS, 3, 8, NC), F32),
            vmem((STREAMS, 17, 8, NC), F32),
            dma((4,)),
            dma((STREAMS, 20)), dma((2, STREAMS, 20)),
            dma((STREAMS, 4)), dma((2, STREAMS, 4)),
            dma((STREAMS, 2)), dma((2, STREAMS, 2)),
            dma((STREAMS, 2, 2)), dma((2, STREAMS, 2, 2)),
            dma((STREAMS,)), dma((2, STREAMS)),
            dma((STREAMS, 17)), dma((STREAMS, 17)),
        ],
        compiler_params=pltpu.CompilerParams(
            collective_id=0, has_side_effects=True, vmem_limit_bytes=67_000_000),
        name="cg_solve",
    )(gram_tiles, right_side)
    step = step[0:1]
    return x + step * d, r - step * s


def solution(mesh):
    return jax.shard_map(
        body,
        mesh=mesh,
        in_specs=(P("rows", "cols"), P(("rows", "cols"), None)),
        out_specs=(P(("rows", "cols"), None), P(("rows", "cols"), None)),
        check_vma=False,
    )
```

```python
import functools

import jax
import jax.numpy as jnp
from jax import lax
from jax.experimental import pallas as pl
from jax.experimental.pallas import tpu as pltpu
from jax.sharding import PartitionSpec as P

ITERS = 4
NX, NZ = 4, 8
PIECE, SLOT, KSLOT = 100, 104, 112
WIDTH = 256
STREAMS = 2
NC = WIDTH // STREAMS
ROWS = 1600
MPAD = 16 * SLOT
KPAD = 16 * KSLOT
CHUNK = 4 * SLOT
F32, BF16 = jnp.float32, jnp.bfloat16

NAMES = ("O0", "O1", "O2", "O3", "O4", "Q0", "Q1", "Q2", "Q3", "Q4")
HALF = (
    "m0",
    "m1",
    "fx",
    "Q0",
    "m2",
    "n0",
    "O2",
    "m3",
    "n1",
    "r0",
    "r1",
    "O3",
    "O4",
    "ox",
    "Q1",
    "Q2",
    "O1",
    "Q3",
    "Q4",
    "up",
    "..",
)
LAST = (
    "f0",
    "m0",
    "m1",
    "fx",
    "m2",
    "n0",
    "m3",
    "n1",
    "r0",
    "r1",
    "f1",
    "ox",
    "f2",
    "up",
)
LOAD = {1: ["Q0"], 3: ["O2", "Q1"]}
TURN = {4: ["O1", "O3", "O4"], 7: ["Q2"], 11: ["Q3"]}
TAIL = ["Q4", ".."]


def halves(x):
    hi = x.astype(BF16)
    lo = (x - hi.astype(F32)).astype(BF16)
    return hi, lo


def follow(names, steps):
    for name in names:
        steps[name]()


def kernel(gram, rhs, ox, od, ores, os_, ostep, tv, tp, t1, t2, tt, vb, ag, os, cr, xa, xs, xb, ys, yr, st, sc, fs, fr,
           t_sem, z_snd, z_rcv, c_snd, c_rcv, xa_snd, xa_rcv, xb_snd, xb_rcv, q_snd, q_rcv,
           f_snd, f_rcv):
    row, col = lax.axis_index("rows"), lax.axis_index("cols")
    xx, yl, core = row // 4, lax.rem(row // 2, 2), lax.rem(row, 2)
    yh, z = col // NZ, lax.rem(col, NZ)

    def at_x(d):
        return (lax.rem(xx + d, NX) * 4 + yl * 2 + core, col)

    def at_z(d):
        return (row, yh * NZ + lax.rem(z + d, NZ))

    at_core = (xx * 4 + yl * 2 + 1 - core, col)
    at_yl = (xx * 4 + (1 - yl) * 2 + core, col)
    at_yh = (row, (1 - yh) * NZ + z)
    at_both = (xx * 4 + (1 - yl) * 2 + 1 - core, col)
    around = [
        [at_core, at_yl, at_both],
        [at_x(d) for d in range(1, NX)] + [at_yh] + [(at_x(d)[0], at_yh[1]) for d in range(1, NX)],
        [at_z(d) for d in range(1, NZ)],
    ]
    partners = around[0] + around[1] + around[2]

    def remote(src, dst, snd, rcv, to):
        return pltpu.make_async_remote_copy(
            src_ref=src, dst_ref=dst, send_sem=snd, recv_sem=rcv, device_id=to,
            device_id_type=pl.DeviceIdType.MESH)

    for m in range(4):
        pltpu.make_async_copy(gram.at[pl.ds(400 * m, 400), :], tv.at[pl.ds(400 * m, 400), :], t_sem.at[m]).start()

    barrier = pltpu.get_barrier_semaphore()
    for to in partners:
        pl.semaphore_signal(barrier, inc=1, device_id=to, device_id_type=pl.DeviceIdType.MESH)

    def slot(kind, d):
        return (yh if kind == 0 else 1 - yh) * NZ + lax.rem(z + d + NZ, NZ)

    def pack(t, s, at):
        x = jnp.concatenate([ag[t, s, at], jnp.zeros((KSLOT - SLOT, NC), F32)], axis=0)
        hi, lo = halves(x)
        start = pl.multiple_of(at * KSLOT, 16)
        vb[s, pl.ds(start, KSLOT), 0:NC] = hi
        vb[s, pl.ds(start, KSLOT), NC:2 * NC] = lo

    def gather(t, s):
        par = lax.rem(t, 2)
        ways = (1, -1)

        def piece(name, way):
            kind, d = (0 if name[0] == "O" else 1), int(name[1])
            return ag.at[t, s, slot(kind, -ways[way] * d)]

        def view(have, way, name):
            src = piece(have, way)
            return src.at[(pl.ds(0, 56), pl.ds(56, 48))[way]] if name[1] == "4" else src

        def index(name, way):
            return NAMES.index(name) * 2 + way

        def copy(have, as_name, way, to):
            src = view(have, way, as_name)
            k = index(as_name, way)
            return remote(src, src, z_snd.at[s, k], z_rcv.at[par, s, k], to)

        def landing(name, way):
            dst = view(name, way, name)
            k = index(name, way)
            return remote(dst, dst, z_snd.at[s, k], z_rcv.at[par, s, k], at_yh)

        def along(way, hops):
            return at_z((ways[way] * hops) % NZ)

        def both(have, as_name, hops):
            return [copy(have, as_name, way, along(way, hops)) for way in range(2)]

        def begin():
            return [copy("O0", "Q0", 0, at_yh)] + both("O0", "O2", 2) + both("O0", "O1", 1)

        sends = lambda: {
            "Q0": [both("Q0", "Q1", 1), []],
            "O2": [[copy("O2", "O3", way, along(way, 1)), copy("O2", "O4", way, along(way, 2)),
                    copy("O2", "Q2", way, at_yh)] for way in range(2)],
            "O3": [[copy("O3", "Q3", 0, at_yh)], [copy("O3", "Q3", 1, at_yh)]],
            "O4": [[copy("O4", "Q4", way, at_yh)] for way in range(2)],
        }

        def first():
            for c in begin():
                c.start()
            pack(t, s, slot(0, 0))

        def take(name, count=2):
            def run():
                onward = sends().get(name, [[], []])
                for way in range(count):
                    landing(name, way).wait_recv()
                    for c in onward[way]:
                        c.start()
                for way in range(1 if name[1] == "4" else count):
                    kind, d = (0 if name[0] == "O" else 1), int(name[1])
                    pack(t, s, slot(kind, -ways[way] * d))
            return run

        def drain():
            for c in begin():
                c.wait_send()
            for group in sends().values():
                for some in group:
                    for c in some:
                        c.wait_send()

        return first, {"Q0": take("Q0", 1), "O2": take("O2"), "Q1": take("Q1"), "O1": take("O1"), "O3": take("O3"),
                       "O4": take("O4"), "Q2": take("Q2"), "Q3": take("Q3"), "Q4": take("Q4"), "..": drain}

    def scatter(t, s, start_next=True):
        par = lax.rem(t, 2)
        ahead = (2, 1, 3, 0)

        def c_copy(e):
            to = lax.rem(xx + ahead[e], NX)
            return remote(os.at[s, to, 1 - core], cr.at[t, s, to], c_snd.at[s, e], c_rcv.at[par, s, e], at_core)

        def xa_copy(k):
            return remote(xs.at[s, 0, k], xa.at[t, s, k], xa_snd.at[s, k], xa_rcv.at[par, s, k], at_x(1 if k == 0 else 3))

        def xb_copy(way, k):
            return remote(xs.at[s, 1 + way, k], xb.at[t, s, way, k], xb_snd.at[s, way, k], xb_rcv.at[par, s, way, k],
                          at_x(1 if way == 0 else 3))

        def q_copy():
            return remote(ys.at[s], yr.at[t, s], q_snd.at[s], q_rcv.at[par, s], at_yl)

        def spare():
            total = jnp.zeros((8, NC), F32)
            for b in range(16):
                total = total + ag[t, s, b, 96:104, :]
            keep = lax.broadcasted_iota(jnp.int32, (8, NC), 0)
            return jnp.where((keep == 4) | (keep == 5), total, 0.0)

        def multiply(e):
            def run():
                to = lax.rem(xx + ahead[e], NX)
                y = jnp.dot(tt[to], vb[s], preferred_element_type=F32)
                dots = spare()
                for q in range(4):
                    lo, hi = q * SLOT, (q + 1) * SLOT
                    piece = (y[lo:hi, :NC] + (y[lo:hi, NC:] + y[CHUNK + lo:CHUNK + hi, :NC])) + y[CHUNK + lo:CHUNK + hi, NC:]
                    os[s, to, q % 2, q // 2, 0:96] = piece[0:96]
                    os[s, to, q % 2, q // 2, 96:104] = piece[96:104] + dots
                c_copy(e).start()
            return run

        def pair(e, k):
            to = lax.rem(xx + ahead[e], NX)
            return os[s, to, core, k] + cr[t, s, to, k]

        def far_x():
            c_copy(0).wait_recv()
            for k in range(2):
                xs[s, 0, k] = pair(0, k)
                xa_copy(k).start()

        def near_x(way):
            def run():
                c_copy(1 + way).wait_recv()
                k = 1 - way
                xs[s, 1 + way, k] = pair(1 + way, k)
                xb_copy(way, k).start()
            return run

        def relay_x(way):
            def run():
                k = way
                both = pair(1 + way, k)
                xa_copy(k).wait_recv()
                xs[s, 1 + way, k] = both + xa[t, s, k]
                xb_copy(way, k).start()
            return run

        def own_x():
            c_copy(3).wait_recv()
            for way in range(2):
                for k in range(2):
                    xb_copy(way, k).wait_recv()
            k = 1 - yl
            ys[s] = (pair(3, k) + xb[t, s, 0, k]) + xb[t, s, 1, k]
            q_copy().start()

        def update():
            k = yl
            part = (pair(3, k) + xb[t, s, 0, k]) + xb[t, s, 1, k]
            q_copy().wait_recv()
            u = part + yr[t, s]
            renew(t, s, u)

        def drain():
            for e in range(4):
                c_copy(e).wait_send()
            for k in range(2):
                xa_copy(k).wait_send()
            for way in range(2):
                for k in range(2):
                    xb_copy(way, k).wait_send()
            q_copy().wait_send()

        def last():
            update()
            if start_next:
                pl.when(t < ITERS - 1)(gather(t + 1, s)[0])
            drain()

        return {"m0": multiply(0), "m1": multiply(1), "m2": multiply(2), "m3": multiply(3), "fx": far_x,
                "n0": near_x(0), "n1": near_x(1), "r0": relay_x(0), "r1": relay_x(1), "ox": own_x, "up": last}

    R, W, Z, S, D, X = range(6)

    def renew(t, s, u):
        q0 = u[0:PIECE]

        @pl.when(t == 0)
        def _():
            st[s, W, 0:PIECE] = q0
            offer(t, s, q0)

        @pl.when(t > 0)
        def _():
            now, product = u[100:101], u[101:102]
            old_now, old_step = sc[s, 0:1], sc[s, 1:2]
            w = st[s, W, 0:PIECE]
            r = st[s, R, 0:PIECE]
            first = t == 1
            beta = jnp.where(first, 0.0, now / old_now)
            step = now / (product - jnp.where(first, 0.0, beta * now / old_step))
            q = jnp.where(first, q0, (w - q0) / old_step)
            zz = q + beta * st[s, Z, 0:PIECE]
            ss = w + beta * st[s, S, 0:PIECE]
            dd = r + beta * st[s, D, 0:PIECE]
            w = w - step * zz
            r = r - step * ss
            sc[s, 0:1] = now
            sc[s, 1:2] = step
            st[s, Z, 0:PIECE] = zz
            st[s, S, 0:PIECE] = ss
            st[s, D, 0:PIECE] = dd
            st[s, W, 0:PIECE] = w
            st[s, R, 0:PIECE] = r
            st[s, X, 0:PIECE] = st[s, X, 0:PIECE] + step * dd

            @pl.when(t < ITERS - 1)
            def _():
                offer(t, s, r - step * w)

    def dots_of(s):
        r = st[s, R, 0:PIECE]
        w = st[s, W, 0:PIECE]
        return jnp.sum(r * r, axis=0, keepdims=True), jnp.sum(r * w, axis=0, keepdims=True)

    def offer(t, s, v):
        a, b = dots_of(s)
        mine = slot(0, 0)
        ag[t + 1, s, mine, 0:PIECE] = v
        ag[t + 1, s, mine, 100:101] = a
        ag[t + 1, s, mine, 101:102] = b
        ag[t + 1, s, mine, 102:104] = jnp.zeros((2, NC), F32)

    def finish(s):
        plan, first = [], 0
        for group in around:
            plan.append([(to, first + k) for k, to in enumerate(group)])
            first += len(group)

        def copies(stage):
            return [remote(fs.at[s, stage], fr.at[s, k], f_snd.at[s, k], f_rcv.at[s, k], to) for to, k in plan[stage]]

        def begin():
            a, b = dots_of(s)
            fs[s, 0, 0:1] = a
            fs[s, 0, 1:2] = b
            fs[s, 0, 2:8] = jnp.zeros((6, NC), F32)
            for c in copies(0):
                c.start()

        def arrived(stage):
            total = fs[s, stage]
            for c, (_, k) in zip(copies(stage), plan[stage]):
                c.wait_recv()
                total = total + fr[s, k]
            return total

        def onward(stage):
            def run():
                fs[s, stage] = arrived(stage - 1)
                for c in copies(stage):
                    c.start()
            return run

        def close():
            total = arrived(len(plan) - 1)
            now, product = total[0:1], total[1:2]
            old_now, old_step = sc[s, 0:1], sc[s, 1:2]
            beta = now / old_now
            step = now / (product - beta * now / old_step)
            w = st[s, W, 0:PIECE]
            r = st[s, R, 0:PIECE]
            ss = w + beta * st[s, S, 0:PIECE]
            dd = r + beta * st[s, D, 0:PIECE]
            cols = slice(s * NC, (s + 1) * NC)
            ox[:, cols] = st[s, X, 0:PIECE]
            od[:, cols] = dd
            ores[:, cols] = r
            os_[:, cols] = ss
            ostep[:, cols] = jnp.broadcast_to(step, (8, NC))
            for stage in range(len(plan)):
                for c in copies(stage):
                    c.wait_send()

        steps = [begin] + [onward(k) for k in range(1, len(plan))] + [close]
        return {"f%d" % i: run for i, run in enumerate(steps)}

    mine = slot(0, 0)
    st[...] = jnp.zeros(st.shape, F32)
    sc[...] = jnp.ones(sc.shape, F32)
    for s in range(STREAMS):
        b = rhs[:, s * NC:(s + 1) * NC]
        st[s, R, 0:PIECE] = b
        ag[0, s, mine, 0:PIECE] = b
        ag[0, s, mine, 100:104] = jnp.zeros((4, NC), F32)
    for a in range(16):
        t2[a * SLOT + PIECE:(a + 1) * SLOT] = jnp.zeros((SLOT - PIECE, 128), F32)
    pl.semaphore_wait(barrier, len(partners))
    begin, events = gather(0, 0)
    begin()

    @pl.loop(0, 4)
    def _(m):
        src = pl.multiple_of(m * 400, 8)
        pltpu.make_async_copy(gram.at[pl.ds(src, 400), :], tv.at[pl.ds(src, 400), :], t_sem.at[m]).wait()
        for p in range(2):
            base = pl.multiple_of(m * 400 + p * 200, 8)
            into = pl.multiple_of(m * 448 + p * 224, 8)
            for lane in range(0, ROWS, 128):
                wide = min(128, ROWS - lane)
                v = tv[pl.ds(base, 200), lane:lane + wide]
                none = jnp.zeros((KSLOT - PIECE, wide), F32)
                tp[pl.ds(into, 224), lane:lane + wide] = jnp.concatenate([v[0:100], none, v[100:200], none], axis=0)
        for when, names in LOAD.items():
            pl.when(m == when)(functools.partial(follow, names, events))


    @pl.loop(0, KPAD // 128)
    def _(kb):
        at = pl.multiple_of(kb * 128, 128)
        for lane in range(0, ROWS, 128):
            wide = min(128, ROWS - lane)
            t1[lane:lane + wide] = tp[pl.ds(at, 128), lane:lane + wide].T
        for a in range(16):
            t2[a * SLOT:a * SLOT + PIECE] = t1[a * PIECE:(a + 1) * PIECE]
        for p in range(8):
            hi, lo = halves(t2[208 * p:208 * (p + 1)])
            start = (p % 2) * 208
            tt[p // 2, start:start + 208, pl.ds(at, 128)] = hi
            tt[p // 2, CHUNK + start:CHUNK + start + 208, pl.ds(at, 128)] = lo
        pl.when(kb == 8)(gather(0, 1)[0])
        for when, names in TURN.items():
            pl.when(kb == when)(functools.partial(follow, names, events))

    follow(TAIL, events)

    @pl.loop(0, STREAMS * ITERS - 1)
    def _(h):
        sm, tm = lax.rem(h, 2), h // 2
        sg, tg = 1 - sm, (h + 1) // 2
        follow(HALF, gather(tg, sg)[1] | scatter(tm, sm))

    ending = finish(0)
    follow(LAST, ending | scatter(ITERS - 1, 1, False))
    other = finish(1)
    follow(["f0"], other)
    follow(["f3"], ending)
    follow(["f1", "f2", "f3"], other)


def body(gram_tiles, right_side):
    shard = jax.ShapeDtypeStruct(right_side.shape, F32)
    dma = pltpu.SemaphoreType.DMA
    vmem = pltpu.VMEM
    spec = pl.BlockSpec(memory_space=pltpu.VMEM)
    x, d, r, s, step = pl.pallas_call(
        kernel,
        out_shape=(shard,) * 4 + (jax.ShapeDtypeStruct((8, right_side.shape[1]), F32),),
        in_specs=[pl.BlockSpec(memory_space=pl.ANY), spec],
        out_specs=(spec,) * 5,
        scratch_shapes=[
            vmem((ROWS, ROWS), F32),
            vmem((KPAD, ROWS), F32),
            vmem((ROWS, 128), F32),
            vmem((MPAD, 128), F32),
            vmem((4, 2 * CHUNK, KPAD), BF16),
            vmem((STREAMS, KPAD, 2 * NC), BF16),
            vmem((ITERS, STREAMS, 16, SLOT, NC), F32),
            vmem((STREAMS, NX, 2, 2, SLOT, NC), F32),
            vmem((ITERS, STREAMS, NX, 2, SLOT, NC), F32),
            vmem((ITERS, STREAMS, 2, SLOT, NC), F32),
            vmem((STREAMS, 3, 2, SLOT, NC), F32),
            vmem((ITERS, STREAMS, 2, 2, SLOT, NC), F32),
            vmem((STREAMS, SLOT, NC), F32),
            vmem((ITERS, STREAMS, SLOT, NC), F32),
            vmem((STREAMS, 6, SLOT, NC), F32),
            vmem((STREAMS, 8, NC), F32),
            vmem((STREAMS, 3, 8, NC), F32),
            vmem((STREAMS, 17, 8, NC), F32),
            dma((4,)),
            dma((STREAMS, 20)), dma((2, STREAMS, 20)),
            dma((STREAMS, 4)), dma((2, STREAMS, 4)),
            dma((STREAMS, 2)), dma((2, STREAMS, 2)),
            dma((STREAMS, 2, 2)), dma((2, STREAMS, 2, 2)),
            dma((STREAMS,)), dma((2, STREAMS)),
            dma((STREAMS, 17)), dma((STREAMS, 17)),
        ],
        compiler_params=pltpu.CompilerParams(
            collective_id=0, has_side_effects=True, vmem_limit_bytes=67_000_000),
        name="cg_solve",
    )(gram_tiles, right_side)
    step = step[0:1]
    return x + step * d, r - step * s


def solution(mesh):
    return jax.shard_map(
        body,
        mesh=mesh,
        in_specs=(P("rows", "cols"), P(("rows", "cols"), None)),
        out_specs=(P(("rows", "cols"), None), P(("rows", "cols"), None)),
        check_vma=False,
    )
```
